256 devices in a mesh: sample: 16 (over y, x), snp: 16 (over z, core).
Axes of the slice: x: 4, y: 4, z: 8, core: 2. Of those that a mesh axis runs over, the one named last changes fastest.
Arguments:
- dosage: bfloat16 [65536, 16384], P('sample', 'snp'), may hold values from 0 to 2, as said below
- allele_mean: float32 [16384], P('snp'), may hold values from 0.1 to 1.9, as said below
- allele_scale: float32 [16384], P('snp'), may hold values from 1.4 to 3.3, as said below
- probes: float32 [192, 65536], P(None, 'sample'), may hold values from -6 to 6
Outputs:
- applied: float32 [192, 65536], P(None, ('sample', 'snp'))
The draws below stay inside these ranges and needn't reach their ends.
Inputs may be any that keep to these rules, and one draw needn't show every extreme that they name: dosage holds only the values 0, 1 and 2. allele_mean is twice an allele frequency between 0.05 and 0.95. allele_scale is 1 / sqrt(allele_mean * (1 - allele_mean / 2)).
All inputs are finite; a program needn't handle non-finite values.
Results may differ from the reference program's by a relative error of at most 0.0058.
Values sent between devices are 32-bit elements; how exact they have to be, the bound alone decides.
A program may use at most 64 MiB of HBM per device.

```python
import jax
import jax.numpy as jnp
from jax import lax

M = 16384
P_SIZE = 192
ROWS = 4096
N = 65536


def permille(key):
    return jax.random.randint(jax.random.fold_in(key, 7), (M,), 50, 950)


def draw_dosage(key, part):
    freq = permille(key)
    draws = jax.random.randint(jax.random.fold_in(key, 11), (N, M), 0, 1000000)
    first = draws // 1000
    second = draws % 1000
    value = (first < freq[None, :]).astype(jnp.float32) + (second < freq[None, :]).astype(jnp.float32)
    return value.astype(jnp.bfloat16)


def draw_allele_mean(key, part):
    return 2.0 * permille(key).astype(jnp.float32) / 1000.0


def draw_allele_scale(key, part):
    share = permille(key).astype(jnp.float32) / 1000.0
    return 1.0 / jnp.sqrt(2.0 * share * (1.0 - share))


def level_of(key, shape, cuts, low, largest):
    def one(position, blocks):
        heights = jax.random.uniform(jax.random.fold_in(jax.random.fold_in(key, 6), position), (blocks,), jnp.float32, low / len(cuts), largest / len(cuts))
        return jnp.repeat(jnp.exp(heights), shape[position] // blocks).reshape((-1,) + (1,) * (len(shape) - position - 1))

    gain = one(*cuts[0])
    for cut in cuts[1:]:
        gain = gain * one(*cut)
    return gain


def centred(own_key, dims, scale, bound, split=(), held_as=jnp.bfloat16):
    factor_of = level_of(own_key, dims, split, -0.22, 0.18) if split else 1.0
    array = jax.random.normal(own_key, dims, jnp.float32) * scale * factor_of
    return jnp.minimum(jnp.maximum(array, -bound), bound).astype(held_as)


def setup_inputs(seed: int = 0) -> dict:
    keys = jax.random.split(jax.random.key(seed), 5)
    return {
        "dosage": draw_dosage(jax.random.fold_in(keys[4], 71), 0),
        "allele_mean": draw_allele_mean(jax.random.fold_in(keys[4], 71), 0),
        "allele_scale": draw_allele_scale(jax.random.fold_in(keys[4], 71), 0),
        "probes": centred(keys[3], (P_SIZE, N), 1.0, 6.0, ((1, 16),), jnp.float32),
    }


def standard_block(dosage, allele_mean, allele_scale, index):
    block = lax.dynamic_slice_in_dim(dosage, (index * ROWS).astype(jnp.int32), ROWS, 0)
    return ((block.astype(jnp.float32) - allele_mean[None, :]) * allele_scale[None, :]).astype(jnp.bfloat16)

def reference(dosage, allele_mean, allele_scale, probes):
    total = dosage.shape[0]
    width = dosage.shape[1]
    count = total // ROWS
    probe_b = probes.astype(jnp.bfloat16)

    def load_part(index):
        genos = standard_block(dosage, allele_mean, allele_scale, index)
        pslice = lax.dynamic_slice_in_dim(probe_b, (index * ROWS).astype(jnp.int32), ROWS, 1)
        return jnp.dot(pslice, genos, preferred_element_type=jnp.float32)
    loads = lax.optimization_barrier(jnp.sum(lax.map(load_part, jnp.arange(count, dtype=jnp.int32)), axis=0))
    loads_b = (loads / jnp.sqrt(jnp.float32(total))).astype(jnp.bfloat16)

    def apply_part(index):
        genos = standard_block(dosage, allele_mean, allele_scale, index)
        return lax.dot_general(loads_b, genos, (((1,), (1,)), ((), ())), preferred_element_type=jnp.float32)
    parts = lax.map(apply_part, jnp.arange(count, dtype=jnp.int32))
    applied = jnp.transpose(parts, (1, 0, 2)).reshape(loads_b.shape[0], total)
    return applied / jnp.sqrt(jnp.float32(width))
```

```python
import functools

import jax
import jax.numpy as jnp
from jax import lax
from jax.experimental import pallas as pl
from jax.experimental.pallas import tpu as pltpu
from jax.sharding import PartitionSpec as P

MESH = pl.DeviceIdType.MESH
SIDE = 4
RING = 8
BLOCKS = 8
CHUNKS = (64, 64, 64)


def kernel(
    chunks, inv_root_n, inv_root_m, dosage, mean, scale, probes, out,
    genos, pf, acc, rs1, r1, rs2, loads, part, cx, zp, zm,
    d_sem, p_sem, xs, xr, cs, cr, zs, zr,
):
    rows = genos.shape[0]
    step = rows // BLOCKS
    snps = genos.shape[1]
    quarter = snps // SIDE
    width = out.shape[1]
    sample = lax.axis_index("sample")
    snp = lax.axis_index("snp")
    y, x = sample // SIDE, sample % SIDE
    z, core = snp // 2, snp % 2

    def along(axis, j):
        if axis == 0:
            return (y * SIDE + (x + j) % SIDE, snp)
        return (((y + j) % SIDE) * SIDE + x, snp)

    sibling = (sample, z * 2 + (1 - core))
    up = (sample, ((z + 1) % RING) * 2 + core)
    down = (sample, ((z + RING - 1) % RING) * 2 + core)

    def d_copy(b):
        rs = pl.ds(pl.multiple_of(b * step, step), step)
        return pltpu.make_async_copy(dosage.at[rs, :], genos.at[rs, :], d_sem.at[b])

    def p_copy(b):
        rs = pl.ds(pl.multiple_of(b * step, step), step)
        return pltpu.make_async_copy(probes.at[:, rs], pf.at[b], p_sem.at[b])

    for b in range(BLOCKS):
        p_copy(b).start()
        d_copy(b).start()

    barrier = pltpu.get_barrier_semaphore()
    peers = [along(a, j) for a in (0, 1) for j in (1, 2, 3)] + [sibling, up, down]
    for peer in peers:
        pl.semaphore_signal(barrier, inc=1, device_id=peer, device_id_type=MESH)

    m = mean[...]
    s = scale[...]
    g = [((jnp.float32(k) - m) * s).astype(jnp.bfloat16) for k in range(3)]
    acc[...] = jnp.zeros_like(acc)

    @pl.loop(0, BLOCKS)
    def _(b):
        p_copy(b).wait()
        d_copy(b).wait()
        rs = pl.ds(pl.multiple_of(b * step, step), step)
        d = genos[rs, :]
        one = jnp.bfloat16(1)
        block = jnp.where(d == one, g[1], jnp.where(d < one, g[0], g[2]))
        genos[rs, :] = block
        acc[...] += jnp.dot(
            pf[b].astype(jnp.bfloat16), block, preferred_element_type=jnp.float32
        )

    pl.semaphore_wait(barrier, len(peers))

    starts = [sum(chunks[:c]) for c in range(len(chunks))]

    def remote(src, dst, send, recv, to):
        return pltpu.make_async_remote_copy(
            src_ref=src, dst_ref=dst, send_sem=send, recv_sem=recv, device_id=to, device_id_type=MESH
        )

    def xy(c, stage):
        lo, n = starts[c], chunks[c]
        n4 = n // SIDE
        l4 = lo // SIDE
        first = c % 2
        iu, iv = (x, y) if first == 0 else (y, x)
        copies = []
        for j in (1, 2, 3):
            if stage == 0:
                to = (iu + j) % SIDE
                src = acc.at[pl.ds(pl.multiple_of(lo + to * n4, 8), n4), :]
                dst = rs1.at[j - 1, pl.ds(l4, n4), :]
                axis = first
            elif stage == 1:
                to = (iv + j) % SIDE
                src = r1.at[pl.ds(l4, n4), pl.ds(pl.multiple_of(to * quarter, quarter), quarter)]
                dst = rs2.at[j - 1, pl.ds(l4, n4), :]
                axis = 1 - first
            elif stage == 2:
                src = loads.at[
                    pl.ds(pl.multiple_of(lo + iu * n4, 8), n4),
                    pl.ds(pl.multiple_of(iv * quarter, quarter), quarter),
                ]
                dst = src
                axis = 1 - first
            else:
                src = loads.at[pl.ds(pl.multiple_of(lo + iu * n4, 8), n4), :]
                dst = src
                axis = first
            copies.append(
                remote(src, dst, xs.at[c, stage, j - 1], xr.at[c, stage, j - 1], along(axis, j))
            )
        return copies

    def core_copy(c):
        rs = pl.ds(starts[c], chunks[c])
        return remote(part.at[1 - core, :, rs, :], cx.at[:, rs, :], cs.at[c], cr.at[c], sibling)

    def ring(c, hop):
        lo, n = starts[c], chunks[c]
        half = n // 2
        if hop == 1:
            ru, rd = pl.ds(lo, half), pl.ds(lo + half, half)
        else:
            ru = rd = pl.ds(lo, n)
        far = RING // 2 + 1 - hop
        return (
            remote(
                part.at[core, (z + far) % RING, ru, :], zp.at[hop - 1, ru, :],
                zs.at[c, hop - 1, 0], zr.at[c, hop - 1, 0], up,
            ),
            remote(
                part.at[core, (z + RING - far) % RING, rd, :], zm.at[hop - 1, rd, :],
                zs.at[c, hop - 1, 1], zr.at[c, hop - 1, 1], down,
            ),
        )

    def run(c, stage):
        lo, n = starts[c], chunks[c]
        n4 = n // SIDE
        l4 = lo // SIDE
        iu, iv = (x, y) if c % 2 == 0 else (y, x)
        own = pl.ds(pl.multiple_of(lo + iu * n4, 8), n4)
        mine = pl.ds(pl.multiple_of(iv * quarter, quarter), quarter)
        q = pl.ds(l4, n4)
        rs = pl.ds(lo, n)
        if stage == 0:
            for copy in xy(c, 0):
                copy.start()
        elif stage == 1:
            for copy in xy(c, 0):
                copy.wait_recv()
            r1[q, :] = acc[own, :] + rs1[0, q, :] + rs1[1, q, :] + rs1[2, q, :]
            for copy in xy(c, 1):
                copy.start()
        elif stage == 2:
            for copy in xy(c, 1):
                copy.wait_recv()
            total = r1[q, mine] + rs2[0, q, :] + rs2[1, q, :] + rs2[2, q, :]
            loads[own, mine] = total * inv_root_n
            for copy in xy(c, 2):
                copy.start()
        elif stage == 3:
            for copy in xy(c, 2):
                copy.wait_recv()
            for copy in xy(c, 3):
                copy.start()
        elif stage == 4:
            for copy in xy(c, 3):
                copy.wait_recv()
            lb = loads[rs, :].astype(jnp.bfloat16)

            @pl.loop(0, RING)
            def _(t):
                cols = pl.ds(pl.multiple_of(t * 2 * width, 2 * width), 2 * width)
                p = lax.dot_general(
                    lb, genos[cols, :], (((1,), (1,)), ((), ())), preferred_element_type=jnp.float32
                )
                part[0, t, rs, :] = p[:, :width]
                part[1, t, rs, :] = p[:, width:]

            core_copy(c).start()
        elif stage == 5:
            core_copy(c).wait_recv()

            @pl.loop(0, RING)
            def _(t):
                part[core, t, rs, :] += cx[t, rs, :]

            for copy in ring(c, 1):
                copy.start()
        elif stage < 9:
            hop = stage - 5
            for copy in ring(c, hop):
                copy.wait_recv()
            half = n // 2
            ru = pl.ds(lo, half) if hop == 1 else rs
            rd = pl.ds(lo + half, half) if hop == 1 else rs
            far = RING // 2 - hop
            part[core, (z + far) % RING, ru, :] += zp[hop - 1, ru, :]
            part[core, (z + RING - far) % RING, rd, :] += zm[hop - 1, rd, :]
            for copy in ring(c, hop + 1):
                copy.start()
        else:
            for copy in ring(c, 4):
                copy.wait_recv()
            out[rs, :] = (part[core, z, rs, :] + zp[3, rs, :] + zm[3, rs, :]) * inv_root_m

    stages = 10
    for t in range(stages + len(chunks) - 1):
        for c in range(len(chunks)):
            if 0 <= t - c < stages:
                run(c, t - c)

    for c in range(len(chunks)):
        for stage in range(4):
            for copy in xy(c, stage):
                copy.wait_send()
        core_copy(c).wait_send()
        for hop in range(1, 5):
            for copy in ring(c, hop):
                copy.wait_send()


def on_device(dosage, allele_mean, allele_scale, probes):
    rows, snps = dosage.shape
    p = probes.shape[0]
    total = rows * lax.axis_size("sample")
    width = snps * lax.axis_size("snp")
    out_cols = rows // lax.axis_size("snp")
    step = rows // BLOCKS
    f32 = jnp.float32
    n = len(CHUNKS)
    body = functools.partial(kernel, CHUNKS, float(total) ** -0.5, float(width) ** -0.5)
    return pl.pallas_call(
        body,
        out_shape=jax.ShapeDtypeStruct((p, out_cols), f32),
        in_specs=[
            pl.BlockSpec(memory_space=pl.ANY),
            pl.BlockSpec(memory_space=pltpu.VMEM),
            pl.BlockSpec(memory_space=pltpu.VMEM),
            pl.BlockSpec(memory_space=pl.ANY),
        ],
        out_specs=pl.BlockSpec(memory_space=pltpu.VMEM),
        scratch_shapes=[
            pltpu.VMEM((rows, snps), jnp.bfloat16),
            pltpu.VMEM((BLOCKS, p, step), f32),
            pltpu.VMEM((p, snps), f32),
            pltpu.VMEM((SIDE - 1, p // SIDE, snps), f32),
            pltpu.VMEM((p // SIDE, snps), f32),
            pltpu.VMEM((SIDE - 1, p // SIDE, snps // SIDE), f32),
            pltpu.VMEM((p, snps), f32),
            pltpu.VMEM((2, RING, p, out_cols), f32),
            pltpu.VMEM((RING, p, out_cols), f32),
            pltpu.VMEM((4, p, out_cols), f32),
            pltpu.VMEM((4, p, out_cols), f32),
            pltpu.SemaphoreType.DMA((BLOCKS,)),
            pltpu.SemaphoreType.DMA((BLOCKS,)),
            pltpu.SemaphoreType.DMA((n, 4, 3)),
            pltpu.SemaphoreType.DMA((n, 4, 3)),
            pltpu.SemaphoreType.DMA((n,)),
            pltpu.SemaphoreType.DMA((n,)),
            pltpu.SemaphoreType.DMA((n, 4, 2)),
            pltpu.SemaphoreType.DMA((n, 4, 2)),
        ],
        compiler_params=pltpu.CompilerParams(
            collective_id=0, has_side_effects=True, vmem_limit_bytes=48 * 1024 * 1024
        ),
        name="relationship",
    )(dosage, allele_mean.reshape(1, -1), allele_scale.reshape(1, -1), probes)


def solution(mesh):
    placed = (P("sample", "snp"), P("snp"), P("snp"), P(None, "sample"))
    return jax.shard_map(
        on_device, mesh=mesh, in_specs=placed, out_specs=P(None, ("sample", "snp")), check_vma=False
    )
```

```python
import functools

import jax
import jax.numpy as jnp
from jax import lax
from jax.experimental import pallas as pl
from jax.experimental.pallas import tpu as pltpu
from jax.sharding import PartitionSpec as P

MESH = pl.DeviceIdType.MESH
SIDE = 4
RING = 8
BLOCKS = 8
UNIT = 32
GROUPS = (4, 2)
ORDER = """
s0 s1 s2 s3 s4 s5 T
q0 q1 q2 q3 q4 q5
r0 r1 r2 r3 r4 r5
p0 10 p1 20 11 30 21 40 31 50 41 51
"""


def kernel(
    inv_root_n, inv_root_m, dosage, mean, scale, probes, out,
    genos, flipped, pf, ms, acc, r1, ex, loads, part, cx, zz,
    d_sem, p_sem, m_sem, xs, xr, cs, cr, zs, zr,
):
    rows, snps = genos.shape
    step = rows // BLOCKS
    width = out.shape[1]
    piece = UNIT // SIDE
    units = acc.shape[0] // UNIT
    sample = lax.axis_index("sample")
    snp = lax.axis_index("snp")
    y, x = sample // SIDE, sample % SIDE
    z, core = snp // 2, snp % 2

    def along(axis, j):
        if axis == "x":
            return (y * SIDE + (x + j) % SIDE, snp)
        return (((y + j) % SIDE) * SIDE + x, snp)

    sibling = (sample, z * 2 + (1 - core))
    up = (sample, ((z + 1) % RING) * 2 + core)
    down = (sample, ((z + RING - 1) % RING) * 2 + core)

    def block(b):
        return pl.ds(pl.multiple_of(b * step, step), step)

    def d_copy(b):
        return pltpu.make_async_copy(dosage.at[block(b), :], genos.at[block(b), :], d_sem.at[b])

    def p_copy(b):
        return pltpu.make_async_copy(probes.at[:, block(b)], pf.at[b], p_sem.at[b])

    def wait(ref, sem):
        pltpu.make_async_copy(ref, ref, sem).wait()

    pltpu.make_async_copy(mean, ms.at[0], m_sem).start()
    pltpu.make_async_copy(scale, ms.at[1], m_sem).start()
    for b in range(BLOCKS):
        p_copy(b).start()
        d_copy(b).start()

    barrier = pltpu.get_barrier_semaphore()
    peers = [along(a, j) for a in "xy" for j in (1, 2, 3)] + [sibling, up, down]
    for peer in peers:
        pl.semaphore_signal(barrier, inc=1, device_id=peer, device_id_type=MESH)

    wait(ms, m_sem)
    g = [((jnp.float32(k) - ms[0]) * ms[1]).astype(jnp.bfloat16) for k in range(3)]
    acc[...] = jnp.zeros_like(acc)

    @pl.loop(0, BLOCKS)
    def _(b):
        p_copy(b).wait()
        d_copy(b).wait()
        d = genos[block(b), :]
        one = jnp.bfloat16(1)
        made = jnp.where(d == one, g[1], jnp.where(d < one, g[0], g[2]))
        genos[block(b), :] = made
        acc[...] += jnp.dot(
            pf[b].astype(jnp.bfloat16), made, preferred_element_type=jnp.float32
        )

    pl.semaphore_wait(barrier, len(peers))

    def send(src, dst, send_sem, recv_sem, to):
        pltpu.make_async_remote_copy(
            src_ref=src, dst_ref=dst, send_sem=send_sem, recv_sem=recv_sem, device_id=to, device_id_type=MESH
        ).start()

    def slot(u):
        return pl.ds(u * piece, piece)

    def rows_of(u, i):
        return pl.ds(pl.multiple_of(u * UNIT + i * piece, 8), piece)

    def place(u):
        return ("x", "y", x, y) if u % 2 == 0 else ("y", "x", y, x)

    def chunk(c):
        return pl.ds(sum(GROUPS[:c]) * UNIT, GROUPS[c] * UNIT)

    def far(k):
        if k == RING // 2 or k == 0:
            return ((z + k) % RING,)
        return ((z + k) % RING, (z + RING - k) % RING)

    def scatter(u):
        first, _, i, _ = place(u)
        for j in (1, 2, 3):
            send(acc.at[rows_of(u, (i + j) % SIDE), :], r1.at[j - 1, slot(u), :], xs.at[0], xr.at[0, u], along(first, j))

    def exchange(u):
        _, second, i, k = place(u)
        wait(r1.at[:, slot(u), :], xr.at[0, u])
        ex[k, slot(u), :] = acc[rows_of(u, i), :] + r1[0, slot(u), :] + r1[1, slot(u), :] + r1[2, slot(u), :]
        for j in (1, 2, 3):
            send(ex.at[k, slot(u), :], ex.at[k, slot(u), :], xs.at[1], xr.at[1, u], along(second, j))

    def gather(u):
        first, _, i, _ = place(u)
        wait(r1.at[:, slot(u), :], xr.at[1, u])
        mine = rows_of(u, i)
        loads[mine, :] = (ex[0, slot(u), :] + ex[1, slot(u), :] + ex[2, slot(u), :] + ex[3, slot(u), :]) * inv_root_n
        for j in (1, 2, 3):
            send(loads.at[mine, :], loads.at[mine, :], xs.at[2], xr.at[2, u], along(first, j))

    def flip():
        for t in range(RING):
            flipped[t] = genos[pl.ds(t * 2 * width, 2 * width), :].T

    def multiply(c):
        for u in range(sum(GROUPS[:c]), sum(GROUPS[: c + 1])):
            wait(r1.at[:, slot(u), :], xr.at[2, u])
        lb = loads[chunk(c), :].astype(jnp.bfloat16)
        for k in (4, 3, 2, 1, 0):
            for t in far(k):
                p = jnp.dot(lb, flipped[t], preferred_element_type=jnp.float32)
                part[0, t, chunk(c), :] = p[:, :width]
                part[1, t, chunk(c), :] = p[:, width:]
            for t in far(k):
                send(part.at[1 - core, t, chunk(c), :], cx.at[t, chunk(c), :], cs, cr.at[c, k], sibling)

    def hop(c, h):
        lo, n = sum(GROUPS[:c]) * UNIT, GROUPS[c] * UNIT
        rs = chunk(c)
        lower, upper = pl.ds(lo, n // 2), pl.ds(lo + n // 2, n // 2)
        k = RING // 2 + 1 - h
        wait(cx.at[pl.ds(0, len(far(k))), rs, :], cr.at[c, k])
        if h == 2:
            wait(zz.at[0, rs, :], zr.at[c, 0])
        elif h > 2:
            wait(zz.at[pl.ds(0, 2), rs, :], zr.at[c, h - 2])
        if h == 1:
            t = far(k)[0]
            part[core, t, rs, :] += cx[t, rs, :]
            send(part.at[core, t, lower, :], zz.at[0, lower, :], zs, zr.at[c, 0], up)
            send(part.at[core, t, upper, :], zz.at[1, upper, :], zs, zr.at[c, 0], down)
            return
        a, b = 2 * h - 4, 2 * h - 3
        if h == 5:
            total = part[core, z, rs, :] + cx[z, rs, :] + zz[a, rs, :] + zz[b, rs, :]
            out[rs, :] = total * inv_root_m
            return
        tu, td = far(k)
        if h == 2:
            part[core, tu, lower, :] += cx[tu, lower, :] + zz[a, lower, :]
            part[core, tu, upper, :] += cx[tu, upper, :]
        else:
            part[core, tu, rs, :] += cx[tu, rs, :] + zz[a, rs, :]
        send(part.at[core, tu, rs, :], zz.at[a + 2, rs, :], zs, zr.at[c, h - 1], up)
        if h == 2:
            part[core, td, lower, :] += cx[td, lower, :]
            part[core, td, upper, :] += cx[td, upper, :] + zz[b, upper, :]
        else:
            part[core, td, rs, :] += cx[td, rs, :] + zz[b, rs, :]
        send(part.at[core, td, rs, :], zz.at[b + 2, rs, :], zs, zr.at[c, h - 1], down)

    tasks = {"s": scatter, "q": exchange, "r": gather, "p": multiply}
    for task in ORDER.split():
        if task == "T":
            flip()
        elif task[0] in tasks:
            tasks[task[0]](int(task[1]))
        else:
            hop(int(task[1]), int(task[0]))

    for i in range(3):
        wait(r1, xs.at[i])
    wait(cx, cs)
    wait(zz.at[pl.ds(0, 7)], zs)


def on_device(dosage, allele_mean, allele_scale, probes):
    rows, snps = dosage.shape
    p = probes.shape[0]
    total = rows * lax.axis_size("sample")
    width = snps * lax.axis_size("snp")
    out_cols = rows // lax.axis_size("snp")
    f32 = jnp.float32
    n = len(GROUPS)
    units = p // UNIT
    body = functools.partial(kernel, float(total) ** -0.5, float(width) ** -0.5)
    dma = pltpu.SemaphoreType.DMA
    return pl.pallas_call(
        body,
        out_shape=jax.ShapeDtypeStruct((p, out_cols), f32),
        in_specs=[pl.BlockSpec(memory_space=pltpu.HBM)] * 4,
        out_specs=pl.BlockSpec(memory_space=pltpu.VMEM),
        scratch_shapes=[
            pltpu.VMEM((rows, snps), jnp.bfloat16),
            pltpu.VMEM((RING, snps, 2 * out_cols), jnp.bfloat16),
            pltpu.VMEM((BLOCKS, p, rows // BLOCKS), f32),
            pltpu.VMEM((2, 1, snps), f32),
            pltpu.VMEM((p, snps), f32),
            pltpu.VMEM((SIDE - 1, p // SIDE, snps), f32),
            pltpu.VMEM((SIDE, p // SIDE, snps), f32),
            pltpu.VMEM((p, snps), f32),
            pltpu.VMEM((2, RING, p, out_cols), f32),
            pltpu.VMEM((RING, p, out_cols), f32),
            pltpu.VMEM((8, p, out_cols), f32),
            dma((BLOCKS,)),
            dma((BLOCKS,)),
            dma(()),
            dma((3,)),
            dma((3, units)),
            dma(()),
            dma((n, 5)),
            dma(()),
            dma((n, 4)),
        ],
        compiler_params=pltpu.CompilerParams(
            collective_id=0, has_side_effects=True, vmem_limit_bytes=56 * 1024 * 1024
        ),
        name="relationship",
    )(dosage, allele_mean.reshape(1, -1), allele_scale.reshape(1, -1), probes)


def solution(mesh):
    placed = (P("sample", "snp"), P("snp"), P("snp"), P(None, "sample"))
    return jax.shard_map(
        on_device, mesh=mesh, in_specs=placed, out_specs=P(None, ("sample", "snp")), check_vma=False
    )
```

```python
import functools

import jax
import jax.numpy as jnp
from jax import lax
from jax.experimental import pallas as pl
from jax.experimental.pallas import tpu as pltpu
from jax.sharding import PartitionSpec as P

MESH = pl.DeviceIdType.MESH
SIDE = 4
RING = 8
BLOCKS = 8
HALVES = 1
UNIT = 32
GROUPS = (4, 2)
TRAINS = ((4,), (2,))
ORDER = (
    "s0", "s1", "s2", "s3", "s4", "s5",
    "t0", "t1", "t2", "t3", "t4", "t5", "t6", "t7",
    "q0", "q1", "q2", "q3", "q4", "q5",
    "r0", "r1", "r2", "r3", "r4", "r5",
    "p0", "10", "p1", "11",
    "20", "21",
    "30", "31",
    "40", "41",
    "50", "51",
)


def kernel(
    inv_root_n, inv_root_m, dosage, mean, scale, probes, out,
    genos, flipped, pf, pb, ms, acc, r1, ex, loads, part, cx, zz,
    d_sem, p_sem, m_sem, xs, sr, xr, cs, cr, zs, zr,
):
    rows, snps = genos.shape
    step = rows // BLOCKS
    span = snps // HALVES
    width = out.shape[1]
    piece = UNIT // SIDE
    units = acc.shape[0] // UNIT
    sample = lax.axis_index("sample")
    snp = lax.axis_index("snp")
    y, x = sample // SIDE, sample % SIDE
    z, core = snp // 2, snp % 2

    def along(axis, j):
        if axis == "x":
            return (y * SIDE + (x + j) % SIDE, snp)
        return (((y + j) % SIDE) * SIDE + x, snp)

    sibling = (sample, z * 2 + (1 - core))
    up = (sample, ((z + 1) % RING) * 2 + core)
    down = (sample, ((z + RING - 1) % RING) * 2 + core)

    def block(b):
        return pl.ds(pl.multiple_of(b * step, step), step)

    def cols(h):
        return pl.ds(h * span, span)

    def d_copy(h, b):
        here = block(b), cols(h)
        return pltpu.make_async_copy(dosage.at[here], genos.at[here], d_sem.at[h, b])

    def p_copy(b):
        return pltpu.make_async_copy(probes.at[:, block(b)], pf.at[b], p_sem.at[b])

    def wait(ref, sem):
        pltpu.make_async_copy(ref, ref, sem).wait()

    pltpu.make_async_copy(mean, ms.at[0], m_sem).start()
    pltpu.make_async_copy(scale, ms.at[1], m_sem).start()
    for h in range(HALVES):
        for b in range(BLOCKS):
            if h == 0:
                p_copy(b).start()
            d_copy(h, b).start()

    barrier = pltpu.get_barrier_semaphore()
    peers = [along(a, j) for a in "xy" for j in (1, 2, 3)] + [sibling, up, down]
    for peer in peers:
        pl.semaphore_signal(barrier, inc=1, device_id=peer, device_id_type=MESH)

    wait(ms, m_sem)
    g = [((jnp.float32(k) - ms[0]) * ms[1]).astype(jnp.bfloat16) for k in range(3)]

    def load(h):
        acc[:, cols(h)] = jnp.zeros((acc.shape[0], span), jnp.float32)

        @pl.loop(0, BLOCKS)
        def _(b):
            if h == 0:
                p_copy(b).wait()
                pb[b] = pf[b].astype(jnp.bfloat16)
            d_copy(h, b).wait()
            d = genos[block(b), cols(h)]
            one = jnp.bfloat16(1)
            g0, g1, g2 = (v[:, h * span : (h + 1) * span] for v in g)
            made = jnp.where(d == one, g1, jnp.where(d < one, g0, g2))
            genos[block(b), cols(h)] = made
            acc[:, cols(h)] += jnp.dot(pb[b], made, preferred_element_type=jnp.float32)

    def send(src, dst, send_sem, recv_sem, to):
        pltpu.make_async_remote_copy(
            src_ref=src, dst_ref=dst, send_sem=send_sem, recv_sem=recv_sem, device_id=to, device_id_type=MESH
        ).start()

    def slot(u):
        return pl.ds(u * piece, piece)

    def rows_of(u, i):
        return pl.ds(pl.multiple_of(u * UNIT + i * piece, 8), piece)

    def place(u):
        return ("x", "y", x, y) if u % 2 == 0 else ("y", "x", y, x)

    def chunk(c):
        return pl.ds(sum(GROUPS[:c]) * UNIT, GROUPS[c] * UNIT)

    def far(k):
        if k == RING // 2 or k == 0:
            return ((z + k) % RING,)
        return ((z + k) % RING, (z + RING - k) % RING)

    def scatter(u, h=HALVES - 1):
        first, _, i, _ = place(u)
        for j in (1, 2, 3):
            src = acc.at[rows_of(u, (i + j) % SIDE), cols(h)]
            send(src, r1.at[j - 1, slot(u), cols(h)], xs.at[0], sr.at[h, u], along(first, j))

    def exchange(u):
        _, second, i, k = place(u)
        for h in range(HALVES):
            wait(r1.at[:, slot(u), cols(h)], sr.at[h, u])
        ex[k, slot(u), :] = acc[rows_of(u, i), :] + r1[0, slot(u), :] + r1[1, slot(u), :] + r1[2, slot(u), :]
        for j in (1, 2, 3):
            send(ex.at[k, slot(u), :], ex.at[k, slot(u), :], xs.at[1], xr.at[0, u], along(second, j))

    def gather(u):
        first, _, i, _ = place(u)
        wait(r1.at[:, slot(u), :], xr.at[0, u])
        mine = rows_of(u, i)
        loads[mine, :] = (ex[0, slot(u), :] + ex[1, slot(u), :] + ex[2, slot(u), :] + ex[3, slot(u), :]) * inv_root_n
        for j in (1, 2, 3):
            send(loads.at[mine, :], loads.at[mine, :], xs.at[2], xr.at[1, u], along(first, j))

    def flip(t):
        flipped[t] = genos[pl.ds(t * 2 * width, 2 * width), :].T

    def multiply(c):
        for u in range(sum(GROUPS[:c]), sum(GROUPS[: c + 1])):
            wait(r1.at[:, slot(u), :], xr.at[1, u])
        lb = loads[chunk(c), :].astype(jnp.bfloat16)
        for k in (4, 3, 2, 1, 0):
            for t in far(k):
                p = jnp.dot(lb, flipped[t], preferred_element_type=jnp.float32)
                part[0, t, chunk(c), :] = p[:, :width]
                part[1, t, chunk(c), :] = p[:, width:]
            for t in far(k):
                send(part.at[1 - core, t, chunk(c), :], cx.at[t, chunk(c), :], cs, cr.at[c, k], sibling)

    trains = []
    for group, parts in enumerate(TRAINS):
        lo = sum(GROUPS[:group]) * UNIT
        for i, part_units in enumerate(parts):
            trains.append((group if i == 0 else None, lo, part_units * UNIT))
            lo += part_units * UNIT

    def hop(c, h):
        group, lo, n = trains[c]
        rs = pl.ds(lo, n)
        lower, upper = pl.ds(lo, n // 2), pl.ds(lo + n // 2, n // 2)
        k = RING // 2 + 1 - h
        if group is not None:
            wait(cx.at[pl.ds(0, len(far(k))), chunk(group), :], cr.at[group, k])
        if h == 2:
            wait(zz.at[0, rs, :], zr.at[c, 0])
        elif h > 2:
            wait(zz.at[pl.ds(0, 2), rs, :], zr.at[c, h - 2])
        if h == 1:
            t = far(k)[0]
            part[core, t, rs, :] += cx[t, rs, :]
            send(part.at[core, t, lower, :], zz.at[0, lower, :], zs, zr.at[c, 0], up)
            send(part.at[core, t, upper, :], zz.at[1, upper, :], zs, zr.at[c, 0], down)
            return
        a, b = 2 * h - 4, 2 * h - 3
        if h == 5:
            total = part[core, z, rs, :] + cx[z, rs, :] + zz[a, rs, :] + zz[b, rs, :]
            out[rs, :] = total * inv_root_m
            return
        tu, td = far(k)
        if h == 2:
            part[core, tu, lower, :] += cx[tu, lower, :] + zz[a, lower, :]
            part[core, tu, upper, :] += cx[tu, upper, :]
        else:
            part[core, tu, rs, :] += cx[tu, rs, :] + zz[a, rs, :]
        send(part.at[core, tu, rs, :], zz.at[a + 2, rs, :], zs, zr.at[c, h - 1], up)
        if h == 2:
            part[core, td, lower, :] += cx[td, lower, :]
            part[core, td, upper, :] += cx[td, upper, :] + zz[b, upper, :]
        else:
            part[core, td, rs, :] += cx[td, rs, :] + zz[b, rs, :]
        send(part.at[core, td, rs, :], zz.at[b + 2, rs, :], zs, zr.at[c, h - 1], down)

    for h in range(HALVES):
        load(h)
        if h == 0:
            pl.semaphore_wait(barrier, len(peers))
        if h < HALVES - 1:
            for u in range(units):
                scatter(u, h)

    tasks = {"t": flip, "s": scatter, "q": exchange, "r": gather, "p": multiply}
    for task in ORDER:
        if task[0] in tasks:
            tasks[task[0]](int(task[1]))
        else:
            hop(int(task[1]), int(task[0]))

    for i in range(3):
        wait(r1, xs.at[i])
    wait(cx, cs)
    wait(zz.at[pl.ds(0, 7)], zs)


def on_device(dosage, allele_mean, allele_scale, probes):
    rows, snps = dosage.shape
    p = probes.shape[0]
    total = rows * lax.axis_size("sample")
    width = snps * lax.axis_size("snp")
    out_cols = rows // lax.axis_size("snp")
    f32 = jnp.float32
    n = len(GROUPS)
    units = p // UNIT
    body = functools.partial(kernel, float(total) ** -0.5, float(width) ** -0.5)
    dma = pltpu.SemaphoreType.DMA
    return pl.pallas_call(
        body,
        out_shape=jax.ShapeDtypeStruct((p, out_cols), f32),
        in_specs=[pl.BlockSpec(memory_space=pltpu.HBM)] * 4,
        out_specs=pl.BlockSpec(memory_space=pltpu.VMEM),
        scratch_shapes=[
            pltpu.VMEM((rows, snps), jnp.bfloat16),
            pltpu.VMEM((RING, snps, 2 * out_cols), jnp.bfloat16),
            pltpu.VMEM((BLOCKS, p, rows // BLOCKS), f32),
            pltpu.VMEM((BLOCKS, p, rows // BLOCKS), jnp.bfloat16),
            pltpu.VMEM((2, 1, snps), f32),
            pltpu.VMEM((p, snps), f32),
            pltpu.VMEM((SIDE - 1, p // SIDE, snps), f32),
            pltpu.VMEM((SIDE, p // SIDE, snps), f32),
            pltpu.VMEM((p, snps), f32),
            pltpu.VMEM((2, RING, p, out_cols), f32),
            pltpu.VMEM((RING, p, out_cols), f32),
            pltpu.VMEM((8, p, out_cols), f32),
            dma((HALVES, BLOCKS)),
            dma((BLOCKS,)),
            dma(()),
            dma((3,)),
            dma((HALVES, units)),
            dma((2, units)),
            dma(()),
            dma((n, 5)),
            dma(()),
            dma((sum(map(len, TRAINS)), 4)),
        ],
        compiler_params=pltpu.CompilerParams(
            collective_id=0, has_side_effects=True, vmem_limit_bytes=52 * 1024 * 1024
        ),
        name="relationship",
    )(dosage, allele_mean.reshape(1, -1), allele_scale.reshape(1, -1), probes)


def solution(mesh):
    placed = (P("sample", "snp"), P("snp"), P("snp"), P(None, "sample"))
    return jax.shard_map(
        on_device, mesh=mesh, in_specs=placed, out_specs=P(None, ("sample", "snp")), check_vma=False
    )
```

```python
import functools

import jax
import jax.numpy as jnp
from jax import lax
from jax.experimental import pallas as pl
from jax.experimental.pallas import tpu as pltpu
from jax.sharding import PartitionSpec as P

MESH = pl.DeviceIdType.MESH
SIDE = 4
RING = 8
BLOCKS = 8
HALVES = 1
UNIT = 32
GROUPS = (4, 2)
TRAINS = ((4,), (2,))
ORDER = (
    "s0", "s1", "s2", "s3", "s4", "s5",
    "t0", "t1", "t2", "t3",
    "q0", "q1", "q2", "q3", "q4", "q5",
    "t4", "t5", "t6", "t7",
    "r0", "r1", "r2", "r3", "r4", "r5",
    "p0", "10", "p1", "11",
    "20", "21",
    "30", "31",
    "40", "41",
    "50", "51",
)


def kernel(
    inv_root_n, inv_root_m, dosage, levels, probes, out,
    genos, flipped, pf, pb, ms, acc, r1, ex, loads, part, cx, zz,
    d_sem, p_sem, m_sem, xs, sr, xr, cs, cr, zs, zr,
):
    rows, snps = genos.shape
    step = rows // BLOCKS
    span = snps // HALVES
    width = out.shape[1]
    piece = UNIT // SIDE
    units = acc.shape[0] // UNIT
    sample = lax.axis_index("sample")
    snp = lax.axis_index("snp")
    y, x = sample // SIDE, sample % SIDE
    z, core = snp // 2, snp % 2

    def along(axis, j):
        if axis == "x":
            return (y * SIDE + (x + j) % SIDE, snp)
        return (((y + j) % SIDE) * SIDE + x, snp)

    sibling = (sample, z * 2 + (1 - core))
    up = (sample, ((z + 1) % RING) * 2 + core)
    down = (sample, ((z + RING - 1) % RING) * 2 + core)

    def block(b):
        return pl.ds(pl.multiple_of(b * step, step), step)

    def cols(h):
        return pl.ds(h * span, span)

    def d_copy(h, b):
        here = block(b), cols(h)
        return pltpu.make_async_copy(dosage.at[here], genos.at[here], d_sem.at[h, b])

    def p_copy(b):
        return pltpu.make_async_copy(probes.at[:, block(b)], pf.at[b], p_sem.at[b])

    def wait(ref, sem):
        pltpu.make_async_copy(ref, ref, sem).wait()

    pltpu.make_async_copy(levels, ms, m_sem).start()
    for h in range(HALVES):
        for b in range(BLOCKS):
            if h == 0:
                p_copy(b).start()
            d_copy(h, b).start()

    barrier = pltpu.get_barrier_semaphore()
    peers = [along(a, j) for a in "xy" for j in (1, 2, 3)] + [sibling, up, down]
    for peer in peers:
        pl.semaphore_signal(barrier, inc=1, device_id=peer, device_id_type=MESH)

    wait(ms, m_sem)
    g = [((jnp.float32(k) - ms[0:1, :]) * ms[1:2, :]).astype(jnp.bfloat16) for k in range(3)]

    def load(h):
        acc[:, cols(h)] = jnp.zeros((acc.shape[0], span), jnp.float32)

        @pl.loop(0, BLOCKS)
        def _(b):
            if h == 0:
                p_copy(b).wait()
                pb[b] = pf[b].astype(jnp.bfloat16)
            d_copy(h, b).wait()
            d = genos[block(b), cols(h)]
            one = jnp.bfloat16(1)
            g0, g1, g2 = (v[:, h * span : (h + 1) * span] for v in g)
            made = jnp.where(d == one, g1, jnp.where(d < one, g0, g2))
            genos[block(b), cols(h)] = made
            acc[:, cols(h)] += jnp.dot(pb[b], made, preferred_element_type=jnp.float32)

    def send(src, dst, send_sem, recv_sem, to):
        pltpu.make_async_remote_copy(
            src_ref=src, dst_ref=dst, send_sem=send_sem, recv_sem=recv_sem, device_id=to, device_id_type=MESH
        ).start()

    def slot(u):
        return pl.ds(u * piece, piece)

    def rows_of(u, i):
        return pl.ds(pl.multiple_of(u * UNIT + i * piece, 8), piece)

    def place(u):
        return ("x", "y", x, y) if u % 2 == 0 else ("y", "x", y, x)

    def chunk(c):
        return pl.ds(sum(GROUPS[:c]) * UNIT, GROUPS[c] * UNIT)

    def far(k):
        if k == RING // 2 or k == 0:
            return ((z + k) % RING,)
        return ((z + k) % RING, (z + RING - k) % RING)

    def scatter(u, h=HALVES - 1):
        first, _, i, _ = place(u)
        for j in (1, 2, 3):
            src = acc.at[rows_of(u, (i + j) % SIDE), cols(h)]
            send(src, r1.at[j - 1, slot(u), cols(h)], xs.at[0], sr.at[h, u], along(first, j))

    def exchange(u):
        _, second, i, k = place(u)
        for h in range(HALVES):
            wait(r1.at[:, slot(u), cols(h)], sr.at[h, u])
        ex[k, slot(u), :] = acc[rows_of(u, i), :] + r1[0, slot(u), :] + r1[1, slot(u), :] + r1[2, slot(u), :]
        for j in (1, 2, 3):
            send(ex.at[k, slot(u), :], ex.at[k, slot(u), :], xs.at[1], xr.at[0, u], along(second, j))

    def gather(u):
        first, _, i, _ = place(u)
        wait(r1.at[:, slot(u), :], xr.at[0, u])
        mine = rows_of(u, i)
        loads[mine, :] = (ex[0, slot(u), :] + ex[1, slot(u), :] + ex[2, slot(u), :] + ex[3, slot(u), :]) * inv_root_n
        for j in (1, 2, 3):
            send(loads.at[mine, :], loads.at[mine, :], xs.at[2], xr.at[1, u], along(first, j))

    def flip(t):
        flipped[t] = genos[pl.ds(t * 2 * width, 2 * width), :].T

    def multiply(c):
        for u in range(sum(GROUPS[:c]), sum(GROUPS[: c + 1])):
            wait(r1.at[:, slot(u), :], xr.at[1, u])
        lb = loads[chunk(c), :].astype(jnp.bfloat16)
        for k in (4, 3, 2, 1, 0):
            for t in far(k):
                p = jnp.dot(lb, flipped[t], preferred_element_type=jnp.float32)
                part[0, t, chunk(c), :] = p[:, :width]
                part[1, t, chunk(c), :] = p[:, width:]
            for t in far(k):
                send(part.at[1 - core, t, chunk(c), :], cx.at[t, chunk(c), :], cs, cr.at[c, k], sibling)

    trains = []
    for group, parts in enumerate(TRAINS):
        lo = sum(GROUPS[:group]) * UNIT
        for i, part_units in enumerate(parts):
            trains.append((group if i == 0 else None, lo, part_units * UNIT))
            lo += part_units * UNIT

    def hop(c, h):
        group, lo, n = trains[c]
        rs = pl.ds(lo, n)
        lower, upper = pl.ds(lo, n // 2), pl.ds(lo + n // 2, n // 2)
        k = RING // 2 + 1 - h
        if group is not None:
            wait(cx.at[pl.ds(0, len(far(k))), chunk(group), :], cr.at[group, k])
        if h == 1:
            t = far(k)[0]
            part[core, t, rs, :] += cx[t, rs, :]
            send(part.at[core, t, lower, :], zz.at[0, lower, :], zs, zr.at[c, 0, 0], up)
            send(part.at[core, t, upper, :], zz.at[1, upper, :], zs, zr.at[c, 0, 1], down)
            return
        a, b = 2 * h - 4, 2 * h - 3

        def arrived(way):
            wait(zz.at[0, lower if h == 2 else rs, :], zr.at[c, h - 2, way])

        arrived(0)
        if h == 5:
            arrived(1)
            total = part[core, z, rs, :] + cx[z, rs, :] + zz[a, rs, :] + zz[b, rs, :]
            out[rs, :] = total * inv_root_m
            return
        tu, td = far(k)
        if h == 2:
            part[core, tu, lower, :] += cx[tu, lower, :] + zz[a, lower, :]
            part[core, tu, upper, :] += cx[tu, upper, :]
        else:
            part[core, tu, rs, :] += cx[tu, rs, :] + zz[a, rs, :]
        send(part.at[core, tu, rs, :], zz.at[a + 2, rs, :], zs, zr.at[c, h - 1, 0], up)
        arrived(1)
        if h == 2:
            part[core, td, lower, :] += cx[td, lower, :]
            part[core, td, upper, :] += cx[td, upper, :] + zz[b, upper, :]
        else:
            part[core, td, rs, :] += cx[td, rs, :] + zz[b, rs, :]
        send(part.at[core, td, rs, :], zz.at[b + 2, rs, :], zs, zr.at[c, h - 1, 1], down)

    for h in range(HALVES):
        load(h)
        if h == 0:
            pl.semaphore_wait(barrier, len(peers))
        if h < HALVES - 1:
            for u in range(units):
                scatter(u, h)

    tasks = {"t": flip, "s": scatter, "q": exchange, "r": gather, "p": multiply}
    for task in ORDER:
        if task[0] in tasks:
            tasks[task[0]](int(task[1]))
        else:
            hop(int(task[1]), int(task[0]))

    for i in range(3):
        wait(r1, xs.at[i])
    wait(cx, cs)
    wait(zz.at[pl.ds(0, 7)], zs)


def on_device(dosage, allele_mean, allele_scale, probes):
    rows, snps = dosage.shape
    p = probes.shape[0]
    total = rows * lax.axis_size("sample")
    width = snps * lax.axis_size("snp")
    out_cols = rows // lax.axis_size("snp")
    f32 = jnp.float32
    n = len(GROUPS)
    units = p // UNIT
    body = functools.partial(kernel, float(total) ** -0.5, float(width) ** -0.5)
    dma = pltpu.SemaphoreType.DMA
    return pl.pallas_call(
        body,
        out_shape=jax.ShapeDtypeStruct((p, out_cols), f32),
        in_specs=[pl.BlockSpec(memory_space=pltpu.HBM)] * 3,
        out_specs=pl.BlockSpec(memory_space=pltpu.VMEM),
        scratch_shapes=[
            pltpu.VMEM((rows, snps), jnp.bfloat16),
            pltpu.VMEM((RING, snps, 2 * out_cols), jnp.bfloat16),
            pltpu.VMEM((BLOCKS, p, rows // BLOCKS), f32),
            pltpu.VMEM((BLOCKS, p, rows // BLOCKS), jnp.bfloat16),
            pltpu.VMEM((2, snps), f32),
            pltpu.VMEM((p, snps), f32),
            pltpu.VMEM((SIDE - 1, p // SIDE, snps), f32),
            pltpu.VMEM((SIDE, p // SIDE, snps), f32),
            pltpu.VMEM((p, snps), f32),
            pltpu.VMEM((2, RING, p, out_cols), f32),
            pltpu.VMEM((RING, p, out_cols), f32),
            pltpu.VMEM((8, p, out_cols), f32),
            dma((HALVES, BLOCKS)),
            dma((BLOCKS,)),
            dma(()),
            dma((3,)),
            dma((HALVES, units)),
            dma((2, units)),
            dma(()),
            dma((n, 5)),
            dma(()),
            dma((sum(map(len, TRAINS)), 4, 2)),
        ],
        compiler_params=pltpu.CompilerParams(
            collective_id=0, has_side_effects=True, vmem_limit_bytes=52 * 1024 * 1024
        ),
        name="relationship",
    )(dosage, jnp.stack([allele_mean, allele_scale]), probes)


def solution(mesh):
    placed = (P("sample", "snp"), P("snp"), P("snp"), P(None, "sample"))
    return jax.shard_map(
        on_device, mesh=mesh, in_specs=placed, out_specs=P(None, ("sample", "snp")), check_vma=False
    )
```

```python
import functools

import jax
import jax.numpy as jnp
from jax import lax
from jax.experimental import pallas as pl
from jax.experimental.pallas import tpu as pltpu
from jax.sharding import PartitionSpec as P

MESH = pl.DeviceIdType.MESH
SIDE = 4
RING = 8
BLOCKS = 8
HALVES = 1
UNIT = 32
GROUPS = (4, 2)
TRAINS = ((4,), (2,))
ORDER = (
    "s0", "s1", "s2", "s3", "s4", "s5",
    "t0", "t1",
    "q0", "q1", "q2", "q3", "q4", "q5",
    "t2", "t3", "t4",
    "r0", "r1", "r2", "r3", "r4", "r5",
    "t5", "t6", "t7",
    "p0", "10", "p1", "11",
    "20", "21",
    "30", "31",
    "40", "41",
    "50", "51",
)


def kernel(
    inv_root_n, inv_root_m, dosage, levels, probes, out,
    genos, flipped, pf, pb, ms, acc, r1, ex, loads, part, cx, zz,
    d_sem, p_sem, m_sem, xs, sr, xr, cs, cr, zs, zr,
):
    rows, snps = genos.shape
    step = rows // BLOCKS
    span = snps // HALVES
    width = out.shape[1]
    piece = UNIT // SIDE
    units = acc.shape[0] // UNIT
    sample = lax.axis_index("sample")
    snp = lax.axis_index("snp")
    y, x = sample // SIDE, sample % SIDE
    z, core = snp // 2, snp % 2

    def along(axis, j):
        if axis == "x":
            return (y * SIDE + (x + j) % SIDE, snp)
        return (((y + j) % SIDE) * SIDE + x, snp)

    sibling = (sample, z * 2 + (1 - core))
    up = (sample, ((z + 1) % RING) * 2 + core)
    down = (sample, ((z + RING - 1) % RING) * 2 + core)

    def block(b):
        return pl.ds(pl.multiple_of(b * step, step), step)

    def cols(h):
        return pl.ds(h * span, span)

    def d_copy(h, b):
        here = block(b), cols(h)
        return pltpu.make_async_copy(dosage.at[here], genos.at[here], d_sem.at[h, b])

    def p_copy(b):
        return pltpu.make_async_copy(probes.at[:, block(b)], pf.at[b], p_sem.at[b])

    def wait(ref, sem):
        pltpu.make_async_copy(ref, ref, sem).wait()

    pltpu.make_async_copy(levels, ms, m_sem).start()
    for h in range(HALVES):
        for b in range(BLOCKS):
            if h == 0:
                p_copy(b).start()
            d_copy(h, b).start()

    barrier = pltpu.get_barrier_semaphore()
    peers = [along(a, j) for a in "xy" for j in (1, 2, 3)] + [sibling, up, down]
    for peer in peers:
        pl.semaphore_signal(barrier, inc=1, device_id=peer, device_id_type=MESH)

    wait(ms, m_sem)
    g = [((jnp.float32(k) - ms[0:1, :]) * ms[1:2, :]).astype(jnp.bfloat16) for k in range(3)]

    def load(h):
        acc[:, cols(h)] = jnp.zeros((acc.shape[0], span), jnp.float32)

        @pl.loop(0, BLOCKS)
        def _(b):
            if h == 0:
                p_copy(b).wait()
                pb[b] = pf[b].astype(jnp.bfloat16)
            d_copy(h, b).wait()
            d = genos[block(b), cols(h)]
            one = jnp.bfloat16(1)
            g0, g1, g2 = (v[:, h * span : (h + 1) * span] for v in g)
            made = jnp.where(d == one, g1, jnp.where(d < one, g0, g2))
            genos[block(b), cols(h)] = made
            acc[:, cols(h)] += jnp.dot(pb[b], made, preferred_element_type=jnp.float32)

    def send(src, dst, send_sem, recv_sem, to):
        pltpu.make_async_remote_copy(
            src_ref=src, dst_ref=dst, send_sem=send_sem, recv_sem=recv_sem, device_id=to, device_id_type=MESH
        ).start()

    def slot(u):
        return pl.ds(u * piece, piece)

    def rows_of(u, i):
        return pl.ds(pl.multiple_of(u * UNIT + i * piece, 8), piece)

    def place(u):
        return ("x", "y", x, y) if u % 2 == 0 else ("y", "x", y, x)

    def chunk(c):
        return pl.ds(sum(GROUPS[:c]) * UNIT, GROUPS[c] * UNIT)

    def far(k):
        if k == RING // 2 or k == 0:
            return ((z + k) % RING,)
        return ((z + k) % RING, (z + RING - k) % RING)

    def scatter(u, h=HALVES - 1):
        first, _, i, _ = place(u)
        for j in (1, 2, 3):
            src = acc.at[rows_of(u, (i + j) % SIDE), cols(h)]
            send(src, r1.at[j - 1, slot(u), cols(h)], xs.at[0], sr.at[h, u], along(first, j))

    def exchange(u):
        _, second, i, k = place(u)
        for h in range(HALVES):
            wait(r1.at[:, slot(u), cols(h)], sr.at[h, u])
        ex[k, slot(u), :] = acc[rows_of(u, i), :] + r1[0, slot(u), :] + r1[1, slot(u), :] + r1[2, slot(u), :]
        for j in (1, 2, 3):
            send(ex.at[k, slot(u), :], ex.at[k, slot(u), :], xs.at[1], xr.at[0, u], along(second, j))

    def gather(u):
        first, _, i, _ = place(u)
        wait(r1.at[:, slot(u), :], xr.at[0, u])
        mine = rows_of(u, i)
        loads[mine, :] = (ex[0, slot(u), :] + ex[1, slot(u), :] + ex[2, slot(u), :] + ex[3, slot(u), :]) * inv_root_n
        for j in (1, 2, 3):
            send(loads.at[mine, :], loads.at[mine, :], xs.at[2], xr.at[1, u], along(first, j))

    def flip(t):
        flipped[t] = genos[pl.ds(t * 2 * width, 2 * width), :].T

    def multiply(c):
        for u in range(sum(GROUPS[:c]), sum(GROUPS[: c + 1])):
            wait(r1.at[:, slot(u), :], xr.at[1, u])
        lb = loads[chunk(c), :].astype(jnp.bfloat16)
        for k in (4, 3, 2, 1, 0):
            for t in far(k):
                p = jnp.dot(lb, flipped[t], preferred_element_type=jnp.float32)
                part[0, t, chunk(c), :] = p[:, :width]
                part[1, t, chunk(c), :] = p[:, width:]
            for t in far(k):
                send(part.at[1 - core, t, chunk(c), :], cx.at[t, chunk(c), :], cs, cr.at[c, k], sibling)

    trains = []
    for group, parts in enumerate(TRAINS):
        lo = sum(GROUPS[:group]) * UNIT
        for i, part_units in enumerate(parts):
            trains.append((group if i == 0 else None, lo, part_units * UNIT))
            lo += part_units * UNIT

    def hop(c, h):
        group, lo, n = trains[c]
        rs = pl.ds(lo, n)
        lower, upper = pl.ds(lo, n // 2), pl.ds(lo + n // 2, n // 2)
        k = RING // 2 + 1 - h
        if group is not None:
            wait(cx.at[pl.ds(0, len(far(k))), chunk(group), :], cr.at[group, k])
        if h == 1:
            t = far(k)[0]
            part[core, t, rs, :] += cx[t, rs, :]
            send(part.at[core, t, lower, :], zz.at[0, lower, :], zs, zr.at[c, 0, 0], up)
            send(part.at[core, t, upper, :], zz.at[1, upper, :], zs, zr.at[c, 0, 1], down)
            return
        a, b = 2 * h - 4, 2 * h - 3

        def arrived(way):
            wait(zz.at[0, lower if h == 2 else rs, :], zr.at[c, h - 2, way])

        arrived(0)
        if h == 5:
            arrived(1)
            total = part[core, z, rs, :] + cx[z, rs, :] + zz[a, rs, :] + zz[b, rs, :]
            out[rs, :] = total * inv_root_m
            return
        tu, td = far(k)
        if h == 2:
            part[core, tu, lower, :] += cx[tu, lower, :] + zz[a, lower, :]
            part[core, tu, upper, :] += cx[tu, upper, :]
        else:
            part[core, tu, rs, :] += cx[tu, rs, :] + zz[a, rs, :]
        send(part.at[core, tu, rs, :], zz.at[a + 2, rs, :], zs, zr.at[c, h - 1, 0], up)
        arrived(1)
        if h == 2:
            part[core, td, lower, :] += cx[td, lower, :]
            part[core, td, upper, :] += cx[td, upper, :] + zz[b, upper, :]
        else:
            part[core, td, rs, :] += cx[td, rs, :] + zz[b, rs, :]
        send(part.at[core, td, rs, :], zz.at[b + 2, rs, :], zs, zr.at[c, h - 1, 1], down)

    for h in range(HALVES):
        load(h)
        if h == 0:
            pl.semaphore_wait(barrier, len(peers))
        if h < HALVES - 1:
            for u in range(units):
                scatter(u, h)

    tasks = {"t": flip, "s": scatter, "q": exchange, "r": gather, "p": multiply}
    for task in ORDER:
        if task[0] in tasks:
            tasks[task[0]](int(task[1]))
        else:
            hop(int(task[1]), int(task[0]))

    for i in range(3):
        wait(r1, xs.at[i])
    wait(cx, cs)
    wait(zz.at[pl.ds(0, 7)], zs)


def on_device(dosage, allele_mean, allele_scale, probes):
    rows, snps = dosage.shape
    p = probes.shape[0]
    total = rows * lax.axis_size("sample")
    width = snps * lax.axis_size("snp")
    out_cols = rows // lax.axis_size("snp")
    f32 = jnp.float32
    n = len(GROUPS)
    units = p // UNIT
    body = functools.partial(kernel, float(total) ** -0.5, float(width) ** -0.5)
    dma = pltpu.SemaphoreType.DMA
    return pl.pallas_call(
        body,
        out_shape=jax.ShapeDtypeStruct((p, out_cols), f32),
        in_specs=[pl.BlockSpec(memory_space=pltpu.HBM)] * 3,
        out_specs=pl.BlockSpec(memory_space=pltpu.VMEM),
        scratch_shapes=[
            pltpu.VMEM((rows, snps), jnp.bfloat16),
            pltpu.VMEM((RING, snps, 2 * out_cols), jnp.bfloat16),
            pltpu.VMEM((BLOCKS, p, rows // BLOCKS), f32),
            pltpu.VMEM((BLOCKS, p, rows // BLOCKS), jnp.bfloat16),
            pltpu.VMEM((2, snps), f32),
            pltpu.VMEM((p, snps), f32),
            pltpu.VMEM((SIDE - 1, p // SIDE, snps), f32),
            pltpu.VMEM((SIDE, p // SIDE, snps), f32),
            pltpu.VMEM((p, snps), f32),
            pltpu.VMEM((2, RING, p, out_cols), f32),
            pltpu.VMEM((RING, p, out_cols), f32),
            pltpu.VMEM((8, p, out_cols), f32),
            dma((HALVES, BLOCKS)),
            dma((BLOCKS,)),
            dma(()),
            dma((3,)),
            dma((HALVES, units)),
            dma((2, units)),
            dma(()),
            dma((n, 5)),
            dma(()),
            dma((sum(map(len, TRAINS)), 4, 2)),
        ],
        compiler_params=pltpu.CompilerParams(
            collective_id=0, has_side_effects=True, vmem_limit_bytes=52 * 1024 * 1024
        ),
        name="relationship",
    )(dosage, jnp.stack([allele_mean, allele_scale]), probes)


def solution(mesh):
    placed = (P("sample", "snp"), P("snp"), P("snp"), P(None, "sample"))
    return jax.shard_map(
        on_device, mesh=mesh, in_specs=placed, out_specs=P(None, ("sample", "snp")), check_vma=False
    )
```
